768 devices in a mesh: pipe: 4 (over y_lo), fsdp: 96 (over x, z, y_hi), tp: 2 (over core).
Axes of the slice: x: 4, y: 8 (y_hi: 2, y_lo: 4; y = y_hi * 4 + y_lo), z: 12, core: 2. Of those that a mesh axis runs over, the one named last changes fastest.
Arguments:
- key_values: bfloat16 [4, 12288, 512], P('pipe', 'fsdp'), may hold values from -6 to 6
- projection: bfloat16 [4, 2, 32832, 128], P('pipe', 'tp', 'fsdp'), may hold values from -0.046875 to 0.046875
- queries: bfloat16 [4, 12288, 4096], P('pipe', 'fsdp'), may hold values from -240 to 240
- out_gradient: bfloat16 [4, 12288, 4096], P('pipe', 'fsdp'), may hold values from -6 to 6
- lengths: int32 [4, 96, 8], P('pipe', 'fsdp'), may hold values from 1 to 64, 128 in all within a row
- counts: int32 [4, 96], P('pipe', 'fsdp'), may hold values from 32 to 128, as said below
Outputs:
- upstream: bfloat16 [4, 12288, 16384], P('pipe', 'fsdp', 'tp')
The draws below stay inside these ranges and needn't reach their ends.
Inputs may be any that keep to these rules, and one draw needn't show every extreme that they name: `counts`: in every phase some data rank has all 128 slots live.
All inputs are finite; a program needn't handle non-finite values.
Results may differ from the reference program's by a relative error of at most 0.0086.
Values may be sent and summed in bfloat16 or wider, within the bound.
A program may use at most 64 MiB of HBM per device.

```python
import math
import jax
import jax.numpy as jnp
import numpy as np
from jax import lax

D = 16384
HD = 128
QH = 16
KVH = 2
TOK_DEV = 128
DOCS = 8
SECTIONS = 4
SPLITS = 2
RANKS = 96
TOKENS = 12288
WSTRIPS = 32832
MOST = 64
N_TP = 2


def draw_queries(key, part):
    first_key = jax.random.fold_in(jax.random.fold_in(key, 11), 0)
    values = jnp.clip(jax.random.normal(first_key, (SECTIONS, TOKENS, KVH * QH * HD), jnp.float32), -6.0, 6.0)
    return values.astype(jnp.bfloat16)


def draw_counts(key, part):
    first_key, second_key = jax.random.split(jax.random.fold_in(key, 23))
    base = jax.random.randint(first_key, (SECTIONS, RANKS), TOK_DEV // 4, TOK_DEV + 1)
    busiest = jax.random.randint(second_key, (SECTIONS,), 0, RANKS)
    marked = jnp.arange(RANKS, dtype=jnp.int32)[None, :] == busiest[:, None]
    return jnp.where(marked, TOK_DEV, base).astype(jnp.int32)


def steps_of(own_key, shape, cuts, low, largest):
    gain, own = 1.0, jax.random.fold_in(own_key, 6)
    for axis_at, blocks in cuts:
        draws = jnp.exp(jax.random.uniform(jax.random.fold_in(own, axis_at), (blocks,), jnp.float32, low / len(cuts), largest / len(cuts)))
        gain = gain * jnp.repeat(draws, shape[axis_at] // blocks).reshape([-1 if axis == axis_at else 1 for axis in range(len(shape))])
    return gain


def profile(count, total, most, skew):
    weights = [(1 << 20) // math.isqrt(standing ** skew) + 1 for standing in range(2, count + 1)]
    surplus, holding = total - most - (count - 1), [1] * (count - 1)
    while surplus > 0:
        candidates = [i for i in range(count - 1) if holding[i] < most]
        whole, left = sum([weights[i] for i in candidates]), surplus
        for i in candidates:
            addition = min(most - holding[i], max(1, left * weights[i] // whole), surplus)
            holding[i] = holding[i] + addition
            surplus = surplus - addition
    return np.array([most] + holding)


def ragged_sizes(rng, number_of, total, reach, lean):
    if number_of == 2:
        one = jax.random.randint(rng, (), max(1, total - reach), min(reach, total - 1) + 1)
        return jnp.stack([one, total - one])
    sizes = jnp.asarray(profile(number_of, total, reach, lean), jnp.int32)
    couples = (number_of - 1) // 2
    source_of, sink = sizes[1:1 + 2 * couples:2], sizes[2:2 + 2 * couples:2]
    margin = jnp.minimum(source_of - 1, reach - sink)
    shifted = jax.random.randint(jax.random.fold_in(rng, 1), (couples,), 0, 1 << 20) % (margin + 1)
    sizes = sizes.at[1:1 + 2 * couples:2].set(source_of - shifted).at[2:2 + 2 * couples:2].set(sink + shifted)
    return sizes[jax.random.permutation(jax.random.fold_in(rng, 2), number_of)]


def scatter_about(rng, dims, spread, most, cuts=(), kind=jnp.bfloat16):
    loudness = steps_of(rng, dims, cuts, -0.22, 0.18) if cuts else 1.0
    values = jax.random.normal(rng, dims, jnp.float32) * spread * loudness
    return jnp.minimum(jnp.maximum(values, -most), most).astype(kind)


def setup_inputs(seed: int = 0) -> dict:
    key_of = jax.random.split(jax.random.key(seed), 7)
    return {
        "key_values": scatter_about(key_of[0], (SECTIONS, TOKENS, KVH * 2 * HD), 1.0, 6.0, ((0, 4), (1, 96))),
        "projection": scatter_about(key_of[1], (SECTIONS, SPLITS, WSTRIPS, 128), D ** -0.5, 0.046875, ((0, 4), (1, 2), (2, 96))),
        "queries": draw_queries(jax.random.fold_in(key_of[6], 71), 0),
        "out_gradient": scatter_about(key_of[3], (SECTIONS, TOKENS, KVH * QH * HD), 1.0, 6.0, ((0, 4), (1, 96))),
        "lengths": jax.vmap(lambda own: ragged_sizes(own, DOCS, TOK_DEV, MOST, 2))(jax.random.split(key_of[4], SECTIONS * RANKS)).reshape((SECTIONS, RANKS, DOCS)).astype(jnp.int32),
        "counts": draw_counts(jax.random.fold_in(key_of[6], 71), 0),
    }


rotary_base = 500000.0


def rotary_tables(positions):
    half_width = HD // 2
    frequency = rotary_base ** (-(jnp.arange(half_width, dtype=jnp.float32) * 2.0 / HD))
    angle = positions.astype(jnp.float32)[:, None] * frequency[None, :]
    return jnp.cos(angle), jnp.sin(angle)


def doc_layout(doc_lengths, live_count, row_count):
    row_index = jnp.arange(row_count, dtype=jnp.int32)
    doc_ends = jnp.cumsum(doc_lengths).astype(jnp.int32)
    segment = jnp.sum((row_index[:, None] >= doc_ends[None, :]).astype(jnp.int32), axis=1).astype(jnp.int32)
    doc_starts = (doc_ends - doc_lengths).astype(jnp.int32)
    doc_index = jnp.arange(doc_lengths.shape[0], dtype=jnp.int32)
    doc_first = jnp.sum(jnp.where(segment[:, None] == doc_index[None, :], doc_starts[None, :], 0), axis=1).astype(jnp.int32)
    positions = (row_index - doc_first).astype(jnp.int32)
    live_rows = row_index < live_count
    allowed = (segment[:, None] == segment[None, :]) & (row_index[None, :] <= row_index[:, None])
    allowed = allowed & live_rows[:, None] & live_rows[None, :]
    return positions, allowed, live_rows


def attend_head(queries, out_gradient, head_kv, cosine_table, sine_table, allowed, live_rows):
    row_count = queries.shape[0]
    score_scale = HD ** -0.5
    raw_keys = head_kv[:, :HD].astype(jnp.float32)
    first_half = raw_keys[:, :HD // 2]
    second_half = raw_keys[:, HD // 2:]
    keys = jnp.concatenate([first_half * cosine_table - second_half * sine_table,
                            second_half * cosine_table + first_half * sine_table], axis=1).astype(jnp.bfloat16)
    values = head_kv[:, HD:].astype(jnp.float32)
    query_heads = queries.reshape(row_count, QH, HD).astype(jnp.float32)
    gradient_heads = out_gradient.reshape(row_count, QH, HD).astype(jnp.float32)
    scores = jnp.einsum("thd,sd->hts", query_heads, keys.astype(jnp.float32)) * score_scale
    masked = jnp.where(allowed[None], scores, -1e30)
    row_top = jnp.max(masked, axis=2, keepdims=True)
    exponent = jnp.where(allowed[None], jnp.exp(masked - row_top), 0.0)
    summed = jnp.sum(exponent, axis=2, keepdims=True)
    summed = jnp.where(live_rows[None, :, None], summed, 1.0)
    soft = exponent / summed
    soft_low = soft.astype(jnp.bfloat16).astype(jnp.float32)
    outputs = jnp.einsum("hts,sd->htd", soft_low, values)
    row_delta = jnp.sum(jnp.transpose(gradient_heads, (1, 0, 2)) * outputs, axis=2, keepdims=True)
    prob_gradient = jnp.einsum("thd,sd->hts", gradient_heads, values)
    score_gradient = (soft * (prob_gradient - row_delta)).astype(jnp.bfloat16).astype(jnp.float32)
    key_gradient = jnp.einsum("hts,thd->sd", score_gradient, query_heads) * score_scale
    value_gradient = jnp.einsum("hts,thd->sd", soft_low, gradient_heads)
    first_grad = key_gradient[:, :HD // 2]
    second_grad = key_gradient[:, HD // 2:]
    return jnp.concatenate([first_grad * cosine_table + second_grad * sine_table,
                            second_grad * cosine_table - first_grad * sine_table,
                            value_gradient], axis=1).astype(jnp.bfloat16)


def attend_rank(rank_items):
    queries, out_gradient, key_values, doc_lengths, live_count = rank_items
    positions, allowed, live_rows = doc_layout(doc_lengths, live_count, queries.shape[0])
    cosine_table, sine_table = rotary_tables(positions)
    pieces = []
    for head in range(KVH):
        pieces.append(attend_head(queries[:, head * QH * HD:(head + 1) * QH * HD],
                                  out_gradient[:, head * QH * HD:(head + 1) * QH * HD],
                                  key_values[:, head * 2 * HD:(head + 1) * 2 * HD],
                                  cosine_table, sine_table, allowed, live_rows))
    return jnp.concatenate(pieces, axis=1)


def phase_backward(phase_items):
    phase_kv, phase_strips, phase_queries, phase_gradient, phase_lengths, phase_counts = phase_items
    half_width = D // N_TP
    columns = KVH * 2 * HD
    weight = phase_strips[:, :half_width * columns // 128, :].reshape(D, columns)
    kv_gradient = lax.map(attend_rank, (
        phase_queries.reshape(RANKS, TOK_DEV, KVH * QH * HD),
        phase_gradient.reshape(RANKS, TOK_DEV, KVH * QH * HD),
        phase_kv.reshape(RANKS, TOK_DEV, columns),
        phase_lengths, phase_counts))
    kv_gradient = kv_gradient.reshape(TOKENS, columns)
    return jnp.dot(kv_gradient, weight.T, preferred_element_type=jnp.float32).astype(jnp.bfloat16)


def reference(key_values, projection, queries, out_gradient, lengths, counts):
    gradients = lax.map(phase_backward, (key_values, projection, queries, out_gradient, lengths, counts))
    return jnp.concatenate([gradients[1:], jnp.zeros_like(gradients[:1])], axis=0)
```

```python
import math

import jax
import jax.numpy as jnp
from jax import lax
from jax.experimental import pallas as pl
from jax.experimental.pallas import tpu as pltpu
from jax.sharding import Mesh
from jax.sharding import PartitionSpec as P

D = 16384
HD = 128
QH = 16
KVH = 2
TOK = 128
DOCS = 8
KV = KVH * 2 * HD
HEAD = QH * HD
NX, NZ, NYH, NYL = 4, 12, 2, 4
STRIPS = 342
ROWS = 88
PAIR = 171
LOCAL = PAIR * NZ
TILE = 128
TILES = 17
HALF = D // 2
ROTARY = 500000.0
READY = ((1, 0, 1), (2, 1, 3), (3, 3, 7), (4, 7, 9), (5, 9, 13), (6, 13, 17))
AXES = ("pipe", "fsdp_0", "fsdp_1", "fsdp_2", "tp")
MESH = pl.DeviceIdType.MESH
F32 = jnp.float32
BF16 = jnp.bfloat16
NT = (((1,), (1,)), ((), ()))


def dot(a, b, dims=(((1,), (0,)), ((), ()))):
    return lax.dot_general(a, b, dims, preferred_element_type=F32)


def iota(shape, dim):
    return lax.broadcasted_iota(jnp.int32, shape, dim)


def at(start, size):
    return pl.ds(pl.multiple_of(start, TILE), size)


def kernel(
    lengths,
    counts,
    kv_hbm,
    strips_hbm,
    q_hbm,
    g_hbm,
    out_hbm,
    kvin,
    strips,
    qbuf,
    gbuf,
    mine,
    piece,
    wp,
    xbuf,
    ybuf,
    rbuf,
    keys,
    masks,
    acc,
    load_sem,
    strip_send,
    strip_recv,
    ring_send,
    ring_recv,
    piece_sem,
    x_send,
    x_recv,
    pair_send,
    pair_recv,
    own_sem,
    y_send,
    y_recv,
    out_sem,
):
    p, x, z, h, c = [lax.axis_index(name) for name in AXES]
    rem, div = lax.rem, lax.div

    def load(src, dst, sem):
        copy = pltpu.make_async_copy(src, dst, load_sem.at[sem])
        copy.start()
        return copy

    strips_in = load(strips_hbm.at[0, 0], strips, 0)
    kv_in = load(kv_hbm.at[0, :, at(c * 2 * HD, 2 * HD)], kvin, 1)
    q_in = load(q_hbm.at[0, :, at(c * HEAD, HEAD)], qbuf, 2)
    g_in = load(g_hbm.at[0, :, at(c * HEAD, HEAD)], gbuf, 3)

    down_p = rem(p + NYL - 1, NYL)
    down_h = rem(h + 1 - div(p + NYL - 1, NYL), NYH)
    up_p = rem(p + 1, NYL)
    up_h = rem(h + div(p + 1, NYL), NYH)
    below = (down_p, x, z, down_h, c)
    far = (down_p, x, z, 1 - down_h, c)
    above = (up_p, x, z, up_h, c)
    far_up = (up_p, x, z, 1 - up_h, c)
    xs = [rem(x + k, NX) for k in range(NX)]
    x_at = [(p, xs[k], z, h, c) for k in range(NX)]
    z_up = (p, x, rem(z + 1, NZ), h, c)
    z_down = (p, x, rem(z + NZ - 1, NZ), h, c)
    partner = (p, x, z, h, 1 - c)

    barrier = pltpu.get_barrier_semaphore()
    friends = (below, far, above, far_up, x_at[1], x_at[2], x_at[3], z_up, z_down, partner)
    for friend in friends:
        pl.semaphore_signal(barrier, inc=1, device_id=friend, device_id_type=MESH)

    strips_in.wait()
    own = strips[...]
    for k in range(4):
        row, col = iota((ROWS, STRIPS), 0), iota((ROWS, STRIPS), 1)
        pick = (col == 4 * row + (k - 2 * h)).astype(F32).astype(BF16)
        mine[:, k * HD : (k + 1) * HD] = dot(pick, own).astype(BF16)

    pl.semaphore_wait(barrier, len(friends))

    sent = []

    def send(src, dst, send_sem, recv_sem, to):
        copy = pltpu.make_async_remote_copy(
            src_ref=src,
            dst_ref=dst,
            send_sem=send_sem,
            recv_sem=recv_sem,
            device_id=to,
            device_id_type=MESH,
        )
        copy.start()
        sent.append(copy)

    def arrived(ref, sem):
        pltpu.make_async_remote_copy(
            src_ref=ref,
            dst_ref=ref,
            send_sem=strip_send.at[0],
            recv_sem=sem,
            device_id=partner,
            device_id_type=MESH,
        ).wait_recv()

    for k, to in enumerate((below, far)):
        send(mine, wp.at[z, h], strip_send.at[k], strip_recv.at[k], to)

    row, col = iota((TOK, TOK), 0), iota((TOK, TOK), 1)
    end = jnp.int32(0)
    row_doc = jnp.zeros((TOK, TOK), jnp.int32)
    col_doc = jnp.zeros((TOK, TOK), jnp.int32)
    row_first = jnp.zeros((TOK, TOK), jnp.int32)
    for k in range(DOCS):
        length = lengths[0, 0, k]
        end = end + length
        past = row >= end
        row_doc = row_doc + past.astype(jnp.int32)
        row_first = row_first + jnp.where(past, length, 0)
        col_doc = col_doc + (col >= end).astype(jnp.int32)
    live = col < counts[0, 0]
    allowed = (row_doc == col_doc) & (row <= col) & live
    masks[0] = allowed.astype(F32)
    masks[1] = live.astype(F32)
    frequency = jnp.exp((col & (HD // 2 - 1)).astype(F32) * (-math.log(ROTARY) * 2.0 / HD))
    angle = (row - row_first).astype(F32) * frequency
    cosine = jnp.cos(angle)
    sine = jnp.sin(angle) * jnp.where(col < HD // 2, -1.0, 1.0)
    kv_in.wait()
    raw = kvin[:, :HD].astype(F32)
    keys[...] = (raw * cosine + pltpu.roll(raw, HD // 2, 1) * sine).astype(BF16)
    masks[2] = cosine
    masks[3] = sine
    acc[...] = jnp.zeros_like(acc)
    q_in.wait()
    g_in.wait()

    def one_head(head):
        scale = HD**-0.5
        q = qbuf[:, at(head * HD, HD)]
        g = gbuf[:, at(head * HD, HD)]
        scores = dot(keys[...], q, NT) * scale
        scores = jnp.where(masks[0] > 0.0, scores, -1e30)
        exponent = jnp.exp(scores - jnp.max(scores, axis=0, keepdims=True))
        summed = jnp.sum(exponent, axis=0, keepdims=True)
        soft = exponent * (masks[1, 0:1, :] / summed)
        low = soft.astype(BF16)
        prob = dot(kvin[:, HD:], g, NT)
        delta = jnp.sum(low.astype(F32) * prob, axis=0, keepdims=True)
        change = (soft * (prob - delta)).astype(BF16)
        return dot(change, q), dot(low, g)

    def some_heads(step, carry):
        parts = [one_head(4 * step + k) for k in range(4)]
        acc[:, :HD] += (parts[0][0] + parts[1][0]) + (parts[2][0] + parts[3][0])
        acc[:, HD:] += (parts[0][1] + parts[1][1]) + (parts[2][1] + parts[3][1])
        return carry

    lax.fori_loop(0, QH // 4, some_heads, 0)
    gradient = acc[:, :HD] * (HD**-0.5)
    turned = gradient * masks[2] - pltpu.roll(gradient, HD // 2, 1) * masks[3]
    wanted = p > 0
    piece[:, :HD] = jnp.where(wanted, turned, 0.0).astype(BF16)
    piece[:, HD:] = jnp.where(wanted, acc[:, HD:], 0.0).astype(BF16)
    cols = at(c * 2 * HD, 2 * HD)
    other_cols = at((1 - c) * 2 * HD, 2 * HD)
    send(piece, xbuf.at[x, :, cols], piece_sem.at[0], piece_sem.at[1], below)

    near_h = rem(h + div(p + 1, NYL), NYH)
    halves = (near_h, 1 - near_h)
    last = ((6, 5), (5, 6))

    def ring(kind, way, step):
        origin = rem(z + NZ - step, NZ) if way == 0 else rem(z + step, NZ)
        block = wp.at[origin, halves[kind]]
        if step == 0:
            if way == 0:
                arrived(block, strip_recv.at[kind])
        else:
            arrived(block, ring_recv.at[kind, way, step])
        if step < last[kind][way]:
            send(
                block,
                block,
                ring_send.at[kind, way, step + 1],
                ring_recv.at[kind, way, step + 1],
                (z_up, z_down)[way],
            )

    ring(0, 0, 0)
    ring(0, 1, 0)
    arrived(xbuf.at[x, :, cols], piece_sem.at[1])
    part = xbuf.at[x, :, cols]
    for k in (1, 3, 2):
        send(part, part, x_send.at[k], x_recv.at[NX - k], x_at[k])
    send(part, part, pair_send.at[0], pair_recv.at[0], partner)
    ring(1, 0, 0)
    ring(1, 1, 0)
    ring(0, 0, 1)
    ring(0, 1, 1)
    for k in (1, 3, 2):
        part = xbuf.at[xs[k], :, cols]
        arrived(part, x_recv.at[k])
        send(part, part, pair_send.at[k], pair_recv.at[k], partner)
    ring(1, 0, 1)
    ring(1, 1, 1)
    for k in range(NX):
        arrived(xbuf.at[xs[k], :, other_cols], pair_recv.at[k])

    def tile(k, carry):
        start = div(17 * z + 8, NZ)
        b = rem(start + 2 * TILES + div(k + 1, 2) * (2 * rem(k, 2) - 1), TILES)
        low = div(3 * b + 3, 4) - 1 + div(16 - b, 16)
        high = low + 1 - div(low + 1, NZ)
        r, i = iota((TILE, ROWS), 0), iota((TILE, ROWS), 1)
        feature = b * TILE - 4 * x + r
        inside = feature < LOCAL
        rows = None
        for m, source in enumerate((low, high)):
            for half in range(2):
                label = i + ((low + m) * PAIR + half * 85)
                pick = ((label == feature) & inside).astype(F32).astype(BF16)
                term = dot(pick, wp[source, half])
                rows = term if rows is None else rows + term
        weight = rows.astype(BF16)
        to = at((x * TILES + b) * TILE, TILE)
        for n in range(NX):
            result = dot(xbuf[xs[n]], weight, NT).astype(BF16)
            if n == 0:
                rbuf[:, to] = result
            else:
                ybuf[k, n - 1] = result
        for n in (2, 1, 3):
            pltpu.make_async_remote_copy(
                src_ref=ybuf.at[k, n - 1],
                dst_ref=rbuf.at[:, to],
                send_sem=y_send.at[n],
                recv_sem=y_recv.at[NX - n],
                device_id=x_at[n],
                device_id_type=MESH,
            ).start()
        return carry

    for step, first, stop in READY:
        if step > 1:
            ring(0, 0, step)
            if step <= last[0][1]:
                ring(0, 1, step)
            if step <= last[1][0]:
                ring(1, 0, step)
            ring(1, 1, step)
        lax.fori_loop(first, stop, tile, 0)

    span = TILES * TILE
    for n in range(1, NX):
        everything = rbuf.at[:, at(xs[n] * span, span)]
        arrived(everything, y_recv.at[n])
    for e in range(NX - 1):
        edge = rbuf[:, (17 * e + 16) * TILE : (17 * e + 17) * TILE]
        rbuf[:, 17 * (e + 1) * TILE : (17 * (e + 1) + 1) * TILE] += edge
    stores = []
    for n in range(NX):
        store = pltpu.make_async_copy(
            rbuf.at[:, n * span : n * span + 16 * TILE],
            out_hbm.at[0, :, n * 16 * TILE : (n + 1) * 16 * TILE],
            out_sem.at[n],
        )
        store.start()
        stores.append(store)
    for copy in sent:
        copy.wait_send()
    for n in range(1, NX):
        everything = rbuf.at[:, 0:span]
        pltpu.make_async_remote_copy(
            src_ref=everything,
            dst_ref=everything,
            send_sem=y_send.at[n],
            recv_sem=y_recv.at[n],
            device_id=x_at[n],
            device_id_type=MESH,
        ).wait_send()
    for store in stores:
        store.wait()


def body(key_values, projection, queries, out_gradient, lengths, counts):
    anywhere = pl.BlockSpec(memory_space=pl.ANY)
    scalars = pl.BlockSpec(memory_space=pltpu.SMEM)
    dma = pltpu.SemaphoreType.DMA
    return pl.pallas_call(
        kernel,
        out_shape=jax.ShapeDtypeStruct((1, TOK, HALF), BF16),
        in_specs=[scalars, scalars, anywhere, anywhere, anywhere, anywhere],
        out_specs=anywhere,
        scratch_shapes=[
            pltpu.VMEM((TOK, 2 * HD), BF16),
            pltpu.VMEM((STRIPS, HD), BF16),
            pltpu.VMEM((TOK, HEAD), BF16),
            pltpu.VMEM((TOK, HEAD), BF16),
            pltpu.VMEM((ROWS, KV), BF16),
            pltpu.VMEM((TOK, 2 * HD), BF16),
            pltpu.VMEM((NZ, NYH, ROWS, KV), BF16),
            pltpu.VMEM((NX, TOK, KV), BF16),
            pltpu.VMEM((TILES, NX - 1, TOK, TILE), BF16),
            pltpu.VMEM((TOK, NX * TILES * TILE), BF16),
            pltpu.VMEM((TOK, HD), BF16),
            pltpu.VMEM((4, TOK, TOK), F32),
            pltpu.VMEM((TOK, 2 * HD), F32),
            dma((4,)),
            dma((2,)),
            dma((2,)),
            dma((2, 2, 7)),
            dma((2, 2, 7)),
            dma((2,)),
            dma((NX,)),
            dma((NX,)),
            dma((NX,)),
            dma((NX,)),
            dma((1,)),
            dma((NX,)),
            dma((NX,)),
            dma((NX,)),
        ],
        compiler_params=pltpu.CompilerParams(collective_id=0, has_side_effects=True),
    )(lengths, counts, key_values, projection, queries, out_gradient)


def solution(mesh):
    split = Mesh(
        mesh.devices.reshape(mesh.shape["pipe"], NX, NZ, NYH, mesh.shape["tp"]),
        AXES,
    )
    fsdp = AXES[1:4]
    return jax.shard_map(
        body,
        mesh=split,
        in_specs=(
            P("pipe", fsdp, None),
            P("pipe", "tp", fsdp, None),
            P("pipe", fsdp, None),
            P("pipe", fsdp, None),
            P("pipe", fsdp, None),
            P("pipe", fsdp),
        ),
        out_specs=P("pipe", fsdp, "tp"),
        check_vma=False,
    )
```
